32 devices in a mesh: shot: 8 (over y, x, core), pair: 4 (over z).
Axes of the slice: x: 2, y: 2, z: 4, core: 2. Of those that a mesh axis runs over, the one named last changes fastest.
Arguments:
- spectra: bfloat16 [2, 128, 128, 1024], P(None, 'shot', None, 'pair'), may hold values from -6 to 6
- shot_weight: float32 [128], P('shot'), may hold values from 0.5 to 2
Outputs:
- virtual_gather: bfloat16 [2, 128, 1024, 1024], P(None, 'shot', 'pair')
The draws below stay inside these ranges and needn't reach their ends.
All inputs are finite; a program needn't handle non-finite values.
Results may differ from the reference program's by a relative error of at most 0.0054.
Values may be sent and summed in bfloat16 or wider, within the bound.
A program may use at most 128 MiB of HBM per device.

```python
import math
import jax
import jax.numpy as jnp
from jax import lax

R = 1024
F = 128
SHOTS = 128


def block_levels(rng, dims, pieces, smallest, high):
    gain, own = 1.0, jax.random.fold_in(rng, 6)
    for axis_at, parts in pieces:
        heights = jnp.exp(jax.random.uniform(jax.random.fold_in(own, axis_at), (parts,), jnp.float32, smallest / len(pieces), high / len(pieces)))
        gain = gain * jnp.repeat(heights, dims[axis_at] // parts).reshape([-1 if axis == axis_at else 1 for axis in range(len(dims))])
    return gain


def gaussian(key, dims, scale, limit, split=(), held_as=jnp.bfloat16):
    entries = jax.random.normal(key, dims, jnp.float32) * scale
    if len(split) > 0:
        entries = block_levels(key, dims, split, -0.22, 0.18) * entries
    return jnp.clip(entries, min=-limit, max=limit).astype(held_as)


def setup_inputs(seed: int = 0) -> dict:
    seeds = jax.random.split(jax.random.key(seed), 3)
    spectra = gaussian(seeds[0], (2, SHOTS, F, R), 1.0, 6.0, ((1, 8), (3, 4)))
    shot_weight = jnp.clip(jnp.exp(math.log(2.0) - 1.3862944 * jax.random.uniform(seeds[1], (SHOTS,), jnp.float32) ** block_levels(seeds[1], (SHOTS,), ((0, 8),), -0.2, 0.2)), 0.5, 2.0)
    return dict(spectra=spectra, shot_weight=shot_weight)


def reference(spectra, shot_weight):
    scaled = (spectra.astype(jnp.float32) * shot_weight[None, :, None, None]).astype(jnp.bfloat16)
    factor = SHOTS ** -0.5
    by_freq = jnp.moveaxis(scaled, 2, 0)

    def frequency_gram(frequency_slab):
        real_part = frequency_slab[0]
        imag_part = frequency_slab[1]
        real_out = jnp.dot(real_part.T, real_part, preferred_element_type=jnp.float32) + jnp.dot(imag_part.T, imag_part, preferred_element_type=jnp.float32)
        imag_out = jnp.dot(real_part.T, imag_part, preferred_element_type=jnp.float32) - jnp.dot(imag_part.T, real_part, preferred_element_type=jnp.float32)
        return (jnp.stack([real_out, imag_out]) * factor).astype(jnp.bfloat16)

    gathers = lax.map(frequency_gram, by_freq)
    return jnp.moveaxis(gathers, 1, 0)
```

```python
import functools

import jax
import jax.numpy as jnp
from jax import lax
from jax.experimental import pallas as pl
from jax.experimental.pallas import tpu as pltpu
from jax.sharding import PartitionSpec as P

MESH = pl.DeviceIdType.MESH


def meet(me, step, count):
    out, bit = 0, 1
    while bit < count:
        out = out + ((me // bit + step // bit) % 2) * bit
        bit *= 2
    return out


def gather_kernel(ns, np_, x_ref, g_ref, a2a_sem, up_sem, down_sem, recv_sem, own_sem):
    s, p = lax.axis_index("shot"), lax.axis_index("pair")
    has_up, has_down = p < np_ - 1, p > 0

    barrier = pltpu.get_barrier_semaphore()

    def hello(t, carry):
        pl.semaphore_signal(barrier, inc=1, device_id=(meet(s, t, ns), p), device_id_type=MESH)
        return carry

    lax.fori_loop(1, ns, hello, 0)

    @pl.when(has_up)
    def _():
        pl.semaphore_signal(barrier, inc=1, device_id=(s, p + 1), device_id_type=MESH)

    @pl.when(has_down)
    def _():
        pl.semaphore_signal(barrier, inc=1, device_id=(s, p - 1), device_id_type=MESH)

    pl.semaphore_wait(barrier, ns - 1 + has_up.astype(jnp.int32) + has_down.astype(jnp.int32))

    def up(q, j, src):
        return pltpu.make_async_remote_copy(
            src_ref=src, dst_ref=g_ref.at[q, j], send_sem=up_sem.at[q, j],
            recv_sem=recv_sem.at[q, j], device_id=(s, p + 1), device_id_type=MESH)

    def down(q, j, src):
        return pltpu.make_async_remote_copy(
            src_ref=src, dst_ref=g_ref.at[q, j], send_sem=down_sem.at[q, j],
            recv_sem=recv_sem.at[q, j], device_id=(s, p - 1), device_id_type=MESH)

    def exchange(t):
        j = meet(s, t, ns)
        return pltpu.make_async_remote_copy(
            src_ref=x_ref.at[j], dst_ref=g_ref.at[p, s], send_sem=a2a_sem.at[t],
            recv_sem=recv_sem.at[p, s], device_id=(j, p), device_id_type=MESH)

    def arrived(q, j):
        pltpu.make_async_copy(g_ref.at[q, j], g_ref.at[q, j], recv_sem.at[q, j]).wait()

    own = pltpu.make_async_copy(x_ref.at[s], g_ref.at[p, s], own_sem)

    @pl.when(has_up)
    def _():
        up(p, s, x_ref.at[s]).start()

    @pl.when(has_down)
    def _():
        down(p, s, x_ref.at[s]).start()

    def send(t, carry):
        exchange(t).start()
        return carry

    lax.fori_loop(1, ns, send, 0)
    own.start()

    def first(t, carry):
        j = meet(s, t, ns)
        arrived(p, j)

        @pl.when(has_up)
        def _():
            up(p, j, g_ref.at[p, j]).start()

        @pl.when(has_down)
        def _():
            down(p, j, g_ref.at[p, j]).start()

        return carry

    lax.fori_loop(1, ns, first, 0)

    def relay(i, carry):
        r, j = i // ns, meet(s, i % ns, ns)

        @pl.when(p >= r)
        def _():
            arrived(p - r, j)

            @pl.when(has_up)
            def _():
                up(p - r, j, g_ref.at[p - r, j]).start()

        @pl.when(p + r < np_)
        def _():
            arrived(p + r, j)

            @pl.when(has_down)
            def _():
                down(p + r, j, g_ref.at[p + r, j]).start()

        return carry

    lax.fori_loop(ns, np_ * ns, relay, 0)

    own.wait()

    def exchanged(t, carry):
        exchange(t).wait_send()
        return carry

    lax.fori_loop(1, ns, exchanged, 0)

    def sent(i, carry):
        q, j = i // ns, i % ns

        @pl.when(has_up & (q <= p))
        def _():
            up(q, j, g_ref.at[q, j]).wait_send()

        @pl.when(has_down & (q >= p))
        def _():
            down(q, j, g_ref.at[q, j]).wait_send()

        return carry

    lax.fori_loop(0, np_ * ns, sent, 0)


def gram_kernel(factor, g_ref, o_ref):
    parts, width = g_ref.shape[0], g_ref.shape[-1]
    rows = g_ref[lax.axis_index("pair"), :, 0]
    swapped = jnp.concatenate([-rows[:, 1:2], rows[:, 0:1]], axis=1)
    left = jnp.concatenate([rows.reshape(-1, width), swapped.reshape(-1, width)], axis=1)
    for q in range(parts):
        right = g_ref[q, :, 0].reshape(-1, width)
        product = lax.dot_general(left, right, (((0,), (0,)), ((), ())), preferred_element_type=jnp.float32)
        product = (product * factor).astype(o_ref.dtype)
        o_ref[0, 0, :, q * width:(q + 1) * width] = product[:width]
        o_ref[1, 0, :, q * width:(q + 1) * width] = product[width:]


def gram(gathered, factor):
    np_, ns, bins, _, depth, width = gathered.shape
    if width % 128 == 0:
        return pl.pallas_call(
            functools.partial(gram_kernel, factor),
            grid=(bins,),
            in_specs=[pl.BlockSpec((np_, ns, 1, 2, depth, width), lambda f: (0, 0, f, 0, 0, 0))],
            out_specs=pl.BlockSpec((2, 1, width, np_ * width), lambda f: (0, f, 0, 0)),
            out_shape=jax.ShapeDtypeStruct((2, bins, width, np_ * width), jnp.bfloat16),
        )(gathered)
    rows = lax.dynamic_index_in_dim(gathered, lax.axis_index("pair"), 0, keepdims=False)
    left = jnp.stack([rows, jnp.stack([-rows[:, :, 1], rows[:, :, 0]], axis=2)])
    product = jnp.einsum("ojfcsa,qjfcsb->ofaqb", left, gathered, preferred_element_type=jnp.float32)
    return (product * factor).astype(jnp.bfloat16).reshape(2, bins, width, np_ * width)


def shards(ns, np_, spectra, shot_weight):
    _, depth, freqs, width = spectra.shape
    bins = freqs // ns
    scaled = (spectra.astype(jnp.float32) * shot_weight[None, :, None, None]).astype(jnp.bfloat16)
    outgoing = scaled.transpose(2, 0, 1, 3).reshape(ns, bins, 2, depth, width)
    gathered = pl.pallas_call(
        functools.partial(gather_kernel, ns, np_),
        out_shape=jax.ShapeDtypeStruct((np_, *outgoing.shape), jnp.bfloat16),
        in_specs=[pl.BlockSpec(memory_space=pl.ANY)],
        out_specs=pl.BlockSpec(memory_space=pl.ANY),
        scratch_shapes=[
            pltpu.SemaphoreType.DMA((ns,)),
            pltpu.SemaphoreType.DMA((np_, ns)),
            pltpu.SemaphoreType.DMA((np_, ns)),
            pltpu.SemaphoreType.DMA((np_, ns)),
            pltpu.SemaphoreType.DMA,
        ],
        compiler_params=pltpu.CompilerParams(collective_id=0, has_side_effects=True),
    )(outgoing)
    return gram(gathered, (depth * ns) ** -0.5)


def solution(mesh):
    return jax.shard_map(
        functools.partial(shards, mesh.shape["shot"], mesh.shape["pair"]),
        mesh=mesh,
        in_specs=(P(None, "shot", None, "pair"), P("shot")),
        out_specs=P(None, "shot", "pair", None),
        check_vma=False,
    )
```

```python
import functools

import jax
import jax.numpy as jnp
from jax import lax
from jax.experimental import pallas as pl
from jax.experimental.pallas import tpu as pltpu
from jax.sharding import PartitionSpec as P

MESH = pl.DeviceIdType.MESH


def meet(me, step, count):
    out, bit = 0, 1
    while bit < count:
        out = out + ((me // bit + step // bit) % 2) * bit
        bit *= 2
    return out


def put_left(f, p, g_ref, left_ref):
    width = g_ref.shape[-1]
    rows = g_ref[p, :, f]
    swapped = jnp.concatenate([-rows[:, 1:2], rows[:, 0:1]], axis=1)
    left = jnp.concatenate([rows.reshape(-1, width), swapped.reshape(-1, width)], axis=1)
    left_ref[f] = left.T


def block_product(f, q, g_ref, left_ref, factor):
    width = g_ref.shape[-1]
    right = g_ref[q, :, f].reshape(-1, width)
    return (jnp.dot(left_ref[f], right, preferred_element_type=jnp.float32) * factor).astype(jnp.bfloat16)


def gather_kernel(ns, np_, factor, fused, x_ref, g_ref, *rest):
    if fused:
        left_ref, o_ref, a2a_sem, up_sem, down_sem, recv_sem, own_sem = rest
    else:
        a2a_sem, up_sem, down_sem, recv_sem, own_sem = rest
    s, p = lax.axis_index("shot"), lax.axis_index("pair")
    bins, width = g_ref.shape[2], g_ref.shape[-1]
    share = -(-bins // ns)
    has_up, has_down = p < np_ - 1, p > 0

    barrier = pltpu.get_barrier_semaphore()

    def hello(t, carry):
        pl.semaphore_signal(barrier, inc=1, device_id=(meet(s, t, ns), p), device_id_type=MESH)
        return carry

    lax.fori_loop(1, ns, hello, 0)

    @pl.when(has_up)
    def _():
        pl.semaphore_signal(barrier, inc=1, device_id=(s, p + 1), device_id_type=MESH)

    @pl.when(has_down)
    def _():
        pl.semaphore_signal(barrier, inc=1, device_id=(s, p - 1), device_id_type=MESH)

    pl.semaphore_wait(barrier, ns - 1 + has_up.astype(jnp.int32) + has_down.astype(jnp.int32))

    def up(q, j, src):
        return pltpu.make_async_remote_copy(
            src_ref=src, dst_ref=g_ref.at[q, j], send_sem=up_sem.at[q, j],
            recv_sem=recv_sem.at[q, j], device_id=(s, p + 1), device_id_type=MESH)

    def down(q, j, src):
        return pltpu.make_async_remote_copy(
            src_ref=src, dst_ref=g_ref.at[q, j], send_sem=down_sem.at[q, j],
            recv_sem=recv_sem.at[q, j], device_id=(s, p - 1), device_id_type=MESH)

    def exchange(t):
        j = meet(s, t, ns)
        return pltpu.make_async_remote_copy(
            src_ref=x_ref.at[j], dst_ref=g_ref.at[p, s], send_sem=a2a_sem.at[t],
            recv_sem=recv_sem.at[p, s], device_id=(j, p), device_id_type=MESH)

    def arrived(q, j):
        pltpu.make_async_copy(g_ref.at[q, j], g_ref.at[q, j], recv_sem.at[q, j]).wait()

    own = pltpu.make_async_copy(x_ref.at[s], g_ref.at[p, s], own_sem)

    @pl.when(has_up)
    def _():
        up(p, s, x_ref.at[s]).start()

    @pl.when(has_down)
    def _():
        down(p, s, x_ref.at[s]).start()

    def send(t, carry):
        exchange(t).start()
        return carry

    lax.fori_loop(1, ns, send, 0)
    own.start()

    def first(t, carry):
        j = meet(s, t, ns)
        arrived(p, j)

        @pl.when(has_up)
        def _():
            up(p, j, g_ref.at[p, j]).start()

        @pl.when(has_down)
        def _():
            down(p, j, g_ref.at[p, j]).start()

        return carry

    lax.fori_loop(1, ns, first, 0)

    own.wait()

    def multiply(f, q):
        product = block_product(f, q, g_ref, left_ref, factor)
        columns = pl.ds(pl.multiple_of(q * width, width), width)
        o_ref[0, f, :, columns] = product[:width]
        o_ref[1, f, :, columns] = product[width:]

    def compute(r, t):
        def one_bin(f, carry):
            @pl.when(r == 0)
            def _():
                put_left(f, p, g_ref, left_ref)
                multiply(f, p)

            @pl.when((r > 0) & (p >= r))
            def _():
                multiply(f, p - r)

            @pl.when((r > 0) & (p + r < np_))
            def _():
                multiply(f, p + r)

            return carry

        lax.fori_loop(jnp.minimum(t * share, bins), jnp.minimum((t + 1) * share, bins), one_bin, 0)

    def relay(i, carry):
        r, j = i // ns, meet(s, i % ns, ns)

        @pl.when(p >= r)
        def _():
            arrived(p - r, j)

            @pl.when(has_up)
            def _():
                up(p - r, j, g_ref.at[p - r, j]).start()

        @pl.when(p + r < np_)
        def _():
            arrived(p + r, j)

            @pl.when(has_down)
            def _():
                down(p + r, j, g_ref.at[p + r, j]).start()

        if fused:
            compute(r - 1, i % ns)
        return carry

    lax.fori_loop(ns, np_ * ns, relay, 0)

    def exchanged(t, carry):
        exchange(t).wait_send()
        return carry

    lax.fori_loop(1, ns, exchanged, 0)

    def sent(i, carry):
        q, j = i // ns, i % ns

        @pl.when(has_up & (q <= p))
        def _():
            up(q, j, g_ref.at[q, j]).wait_send()

        @pl.when(has_down & (q >= p))
        def _():
            down(q, j, g_ref.at[q, j]).wait_send()

        return carry

    lax.fori_loop(0, np_ * ns, sent, 0)


def finish_kernel(np_, factor, g_ref, left_ref, o_ref, out_ref, last_ref, done_sem, last_sem):
    p = lax.axis_index("pair")
    bins, width = g_ref.shape[2], g_ref.shape[-1]
    at_end = (p == 0) | (p == np_ - 1)
    q = np_ - 1 - p

    def whole(f):
        return pltpu.make_async_copy(o_ref.at[:, f], out_ref.at[:, f], done_sem.at[f])

    def most(f):
        columns = pl.ds(pl.multiple_of(jnp.where(p == 0, 0, width), width), (np_ - 1) * width)
        return pltpu.make_async_copy(o_ref.at[:, f, :, columns], out_ref.at[:, f, :, columns], done_sem.at[f])

    def last(f):
        columns = pl.ds(pl.multiple_of(q * width, width), width)
        return pltpu.make_async_copy(last_ref.at[:, f], out_ref.at[:, f, :, columns], last_sem.at[f])

    @pl.when(at_end)
    def _():
        for f in range(bins):
            most(f).start()
        for f in range(bins):
            product = block_product(f, q, g_ref, left_ref, factor)
            last_ref[0, f] = product[:width]
            last_ref[1, f] = product[width:]
            if f > 0:
                last(f - 1).start()
        last(bins - 1).start()
        for f in range(bins):
            most(f).wait()
            last(f).wait()

    @pl.when(jnp.logical_not(at_end))
    def _():
        for f in range(bins):
            whole(f).start()
        for f in range(bins):
            whole(f).wait()


def finish(np_, factor, gathered, left, products):
    _, bins, width, columns = products.shape
    return pl.pallas_call(
        functools.partial(finish_kernel, np_, factor),
        out_shape=jax.ShapeDtypeStruct(products.shape, jnp.bfloat16),
        in_specs=[pl.BlockSpec(memory_space=pltpu.VMEM)] * 3,
        out_specs=pl.BlockSpec(memory_space=pl.ANY),
        scratch_shapes=[
            pltpu.VMEM((2, bins, width, width), jnp.bfloat16),
            pltpu.SemaphoreType.DMA((bins,)),
            pltpu.SemaphoreType.DMA((bins,)),
        ],
        compiler_params=pltpu.CompilerParams(vmem_limit_bytes=16 * 2**20),
    )(*(pltpu.with_memory_space_constraint(a, pltpu.VMEM) for a in (gathered, left, products)))


def gram(gathered, factor):
    np_, ns, bins, _, depth, width = gathered.shape
    rows = lax.dynamic_index_in_dim(gathered, lax.axis_index("pair"), 0, keepdims=False)
    left = jnp.stack([rows, jnp.stack([-rows[:, :, 1], rows[:, :, 0]], axis=2)])
    product = jnp.einsum("ojfcsa,qjfcsb->ofaqb", left, gathered, preferred_element_type=jnp.float32)
    return (product * factor).astype(jnp.bfloat16).reshape(2, bins, width, np_ * width)


def shards(ns, np_, spectra, shot_weight):
    _, depth, freqs, width = spectra.shape
    bins = freqs // ns
    scaled = (spectra.astype(jnp.float32) * shot_weight[None, :, None, None]).astype(jnp.bfloat16)
    outgoing = scaled.transpose(2, 0, 1, 3).reshape(ns, bins, 2, depth, width)
    factor = (depth * ns) ** -0.5
    fused = width % 128 == 0
    shapes = [(np_, ns, bins, 2, depth, width)]
    if fused:
        shapes += [(bins, 2 * width, ns * 2 * depth), (2, bins, width, np_ * width)]
    place = pltpu.VMEM if fused else pl.ANY
    results = pl.pallas_call(
        functools.partial(gather_kernel, ns, np_, factor, fused),
        out_shape=[pltpu.VMEM(n, jnp.bfloat16) if fused else jax.ShapeDtypeStruct(n, jnp.bfloat16) for n in shapes],
        in_specs=[pl.BlockSpec(memory_space=pl.ANY)],
        out_specs=[pl.BlockSpec(memory_space=place)] * len(shapes),
        scratch_shapes=[
            pltpu.SemaphoreType.DMA((ns,)),
            pltpu.SemaphoreType.DMA((np_, ns)),
            pltpu.SemaphoreType.DMA((np_, ns)),
            pltpu.SemaphoreType.DMA((np_, ns)),
            pltpu.SemaphoreType.DMA,
        ],
        compiler_params=pltpu.CompilerParams(
            collective_id=0, has_side_effects=True, vmem_limit_bytes=16 * 2**20),
    )(outgoing)
    if fused:
        return finish(np_, factor, *results)
    return gram(results[0], factor)


def solution(mesh):
    return jax.shard_map(
        functools.partial(shards, mesh.shape["shot"], mesh.shape["pair"]),
        mesh=mesh,
        in_specs=(P(None, "shot", None, "pair"), P("shot")),
        out_specs=P(None, "shot", "pair", None),
        check_vma=False,
    )
```

```python
import functools

import jax
import jax.numpy as jnp
from jax import lax
from jax.experimental import pallas as pl
from jax.experimental.pallas import tpu as pltpu
from jax.sharding import PartitionSpec as P

MESH = pl.DeviceIdType.MESH


def meet(me, step, count):
    out, bit = 0, 1
    while bit < count:
        out = out + ((me // bit + step // bit) % 2) * bit
        bit *= 2
    return out


def put_left(f, p, g_ref, left_ref):
    width = g_ref.shape[-1]
    rows = g_ref[p, :, f]
    swapped = jnp.concatenate([-rows[:, 1:2], rows[:, 0:1]], axis=1)
    left = jnp.concatenate([rows.reshape(-1, width), swapped.reshape(-1, width)], axis=1)
    left_ref[f] = left.T


def block_product(f, q, g_ref, left_ref, factor):
    width = g_ref.shape[-1]
    right = g_ref[q, :, f].reshape(-1, width)
    return (jnp.dot(left_ref[f], right, preferred_element_type=jnp.float32) * factor).astype(jnp.bfloat16)


def prepare(t, j, raw_ref, weight_ref, wide_ref, x_ref):
    _, _, depth, bins, width = raw_ref.shape
    for c in range(2):
        for k in range(depth):
            scaled = raw_ref[t, c, k].astype(jnp.float32) * weight_ref[k]
            for h in range(width // 128):
                wide_ref[h, pl.ds((c * depth + k) * bins, bins), :] = scaled[:, h * 128:(h + 1) * 128]
    for c in range(2):
        for f in range(bins):
            for h in range(width // 128):
                shots = wide_ref[h, pl.ds(c * depth * bins + f, depth, stride=bins), :]
                x_ref[j, f, c, :, h * 128:(h + 1) * 128] = shots.astype(jnp.bfloat16)


def gather_kernel(ns, np_, factor, fused, *refs):
    if fused:
        spectra_ref, weight_ref, g_ref, left_ref, o_ref, x_ref, raw_ref, wide_ref, load_sem, *sems = refs
    else:
        x_ref, g_ref, *sems = refs
    a2a_sem, up_sem, down_sem, recv_sem, own_sem = sems
    s, p = lax.axis_index("shot"), lax.axis_index("pair")
    bins, width = g_ref.shape[2], g_ref.shape[-1]
    share = -(-bins // ns)
    has_up, has_down = p < np_ - 1, p > 0

    barrier = pltpu.get_barrier_semaphore()

    def hello(t, carry):
        pl.semaphore_signal(barrier, inc=1, device_id=(meet(s, t, ns), p), device_id_type=MESH)
        return carry

    lax.fori_loop(1, ns, hello, 0)

    @pl.when(has_up)
    def _():
        pl.semaphore_signal(barrier, inc=1, device_id=(s, p + 1), device_id_type=MESH)

    @pl.when(has_down)
    def _():
        pl.semaphore_signal(barrier, inc=1, device_id=(s, p - 1), device_id_type=MESH)

    def load(t):
        first_bin = pl.multiple_of(meet(s, t, ns) * bins, bins)
        return pltpu.make_async_copy(spectra_ref.at[:, :, pl.ds(first_bin, bins), :], raw_ref.at[t], load_sem.at[t])

    def ready(t):
        load(t).wait()
        prepare(t, meet(s, t, ns), raw_ref, weight_ref, wide_ref, x_ref)

    if fused:
        for t in range(ns):
            load(t).start()
        lax.fori_loop(0, min(2, ns), lambda t, carry: (ready(t), carry)[1], 0)

    pl.semaphore_wait(barrier, ns - 1 + has_up.astype(jnp.int32) + has_down.astype(jnp.int32))

    def up(q, j, src):
        return pltpu.make_async_remote_copy(
            src_ref=src, dst_ref=g_ref.at[q, j], send_sem=up_sem.at[q, j],
            recv_sem=recv_sem.at[q, j], device_id=(s, p + 1), device_id_type=MESH)

    def down(q, j, src):
        return pltpu.make_async_remote_copy(
            src_ref=src, dst_ref=g_ref.at[q, j], send_sem=down_sem.at[q, j],
            recv_sem=recv_sem.at[q, j], device_id=(s, p - 1), device_id_type=MESH)

    def exchange(t):
        j = meet(s, t, ns)
        return pltpu.make_async_remote_copy(
            src_ref=x_ref.at[j], dst_ref=g_ref.at[p, s], send_sem=a2a_sem.at[t],
            recv_sem=recv_sem.at[p, s], device_id=(j, p), device_id_type=MESH)

    def arrived(q, j):
        pltpu.make_async_copy(g_ref.at[q, j], g_ref.at[q, j], recv_sem.at[q, j]).wait()

    own = pltpu.make_async_copy(x_ref.at[s], g_ref.at[p, s], own_sem)

    @pl.when(has_up)
    def _():
        up(p, s, x_ref.at[s]).start()

    @pl.when(has_down)
    def _():
        down(p, s, x_ref.at[s]).start()

    def send(t, carry):
        if fused:
            @pl.when(t + 1 < ns)
            def _():
                ready(t + 1)

        exchange(t).start()
        return carry

    lax.fori_loop(1, ns, send, 0)
    own.start()

    def first(t, carry):
        j = meet(s, t, ns)
        arrived(p, j)

        @pl.when(has_up)
        def _():
            up(p, j, g_ref.at[p, j]).start()

        @pl.when(has_down)
        def _():
            down(p, j, g_ref.at[p, j]).start()

        return carry

    lax.fori_loop(1, ns, first, 0)

    own.wait()

    def multiply(f, q):
        product = block_product(f, q, g_ref, left_ref, factor)
        columns = pl.ds(pl.multiple_of(q * width, width), width)
        o_ref[0, f, :, columns] = product[:width]
        o_ref[1, f, :, columns] = product[width:]

    def compute(r, t):
        def one_bin(f, carry):
            @pl.when(r == 0)
            def _():
                put_left(f, p, g_ref, left_ref)
                multiply(f, p)

            @pl.when((r > 0) & (p >= r))
            def _():
                multiply(f, p - r)

            @pl.when((r > 0) & (p + r < np_))
            def _():
                multiply(f, p + r)

            return carry

        lax.fori_loop(jnp.minimum(t * share, bins), jnp.minimum((t + 1) * share, bins), one_bin, 0)

    def relay(i, carry):
        r, j = i // ns, meet(s, i % ns, ns)

        @pl.when(p >= r)
        def _():
            arrived(p - r, j)

            @pl.when(has_up)
            def _():
                up(p - r, j, g_ref.at[p - r, j]).start()

        @pl.when(p + r < np_)
        def _():
            arrived(p + r, j)

            @pl.when(has_down)
            def _():
                down(p + r, j, g_ref.at[p + r, j]).start()

        if fused:
            compute(r - 1, i % ns)
        return carry

    lax.fori_loop(ns, np_ * ns, relay, 0)

    def exchanged(t, carry):
        exchange(t).wait_send()
        return carry

    lax.fori_loop(1, ns, exchanged, 0)

    def sent(i, carry):
        q, j = i // ns, i % ns

        @pl.when(has_up & (q <= p))
        def _():
            up(q, j, g_ref.at[q, j]).wait_send()

        @pl.when(has_down & (q >= p))
        def _():
            down(q, j, g_ref.at[q, j]).wait_send()

        return carry

    lax.fori_loop(0, np_ * ns, sent, 0)


def finish_kernel(np_, factor, g_ref, left_ref, o_ref, out_ref, last_ref, done_sem, last_sem):
    p = lax.axis_index("pair")
    bins, width = g_ref.shape[2], g_ref.shape[-1]
    at_end = (p == 0) | (p == np_ - 1)
    q = np_ - 1 - p

    def whole(f):
        return pltpu.make_async_copy(o_ref.at[:, f], out_ref.at[:, f], done_sem.at[f])

    def most(f):
        columns = pl.ds(pl.multiple_of(jnp.where(p == 0, 0, width), width), (np_ - 1) * width)
        return pltpu.make_async_copy(o_ref.at[:, f, :, columns], out_ref.at[:, f, :, columns], done_sem.at[f])

    def last(f):
        columns = pl.ds(pl.multiple_of(q * width, width), width)
        return pltpu.make_async_copy(last_ref.at[:, f], out_ref.at[:, f, :, columns], last_sem.at[f])

    @pl.when(at_end)
    def _():
        for f in range(bins):
            most(f).start()
        for f in range(bins):
            product = block_product(f, q, g_ref, left_ref, factor)
            last_ref[0, f] = product[:width]
            last_ref[1, f] = product[width:]
            if f > 0:
                last(f - 1).start()
        last(bins - 1).start()
        for f in range(bins):
            most(f).wait()
            last(f).wait()

    @pl.when(jnp.logical_not(at_end))
    def _():
        for f in range(bins):
            whole(f).start()
        for f in range(bins):
            whole(f).wait()


def finish(np_, factor, gathered, left, products):
    _, bins, width, columns = products.shape
    return pl.pallas_call(
        functools.partial(finish_kernel, np_, factor),
        out_shape=jax.ShapeDtypeStruct(products.shape, jnp.bfloat16),
        in_specs=[pl.BlockSpec(memory_space=pltpu.VMEM)] * 3,
        out_specs=pl.BlockSpec(memory_space=pl.ANY),
        scratch_shapes=[
            pltpu.VMEM((2, bins, width, width), jnp.bfloat16),
            pltpu.SemaphoreType.DMA((bins,)),
            pltpu.SemaphoreType.DMA((bins,)),
        ],
        compiler_params=pltpu.CompilerParams(vmem_limit_bytes=16 * 2**20),
    )(*(pltpu.with_memory_space_constraint(a, pltpu.VMEM) for a in (gathered, left, products)))


def gram(gathered, factor):
    np_, ns, bins, _, depth, width = gathered.shape
    rows = lax.dynamic_index_in_dim(gathered, lax.axis_index("pair"), 0, keepdims=False)
    left = jnp.stack([rows, jnp.stack([-rows[:, :, 1], rows[:, :, 0]], axis=2)])
    product = jnp.einsum("ojfcsa,qjfcsb->ofaqb", left, gathered, preferred_element_type=jnp.float32)
    return (product * factor).astype(jnp.bfloat16).reshape(2, bins, width, np_ * width)


def shards(ns, np_, spectra, shot_weight):
    _, depth, freqs, width = spectra.shape
    bins = freqs // ns
    factor = (depth * ns) ** -0.5
    fused = width % 128 == 0 and bins % 16 == 0 and depth % 16 == 0
    shapes = [(np_, ns, bins, 2, depth, width)]
    if fused:
        shapes += [(bins, 2 * width, ns * 2 * depth), (2, bins, width, np_ * width)]
        operands = tuple(pltpu.with_memory_space_constraint(a, pltpu.HBM) for a in (spectra, shot_weight))
        in_specs = [pl.BlockSpec(memory_space=pltpu.HBM), pl.BlockSpec(memory_space=pltpu.SMEM)]
        scratch = [
            pltpu.VMEM((ns, bins, 2, depth, width), jnp.bfloat16),
            pltpu.VMEM((ns, 2, depth, bins, width), jnp.bfloat16),
            pltpu.VMEM((width // 128, 2 * depth * bins, 128), jnp.float32),
            pltpu.SemaphoreType.DMA((ns,)),
        ]
    else:
        scaled = (spectra.astype(jnp.float32) * shot_weight[None, :, None, None]).astype(jnp.bfloat16)
        operands = (scaled.transpose(2, 0, 1, 3).reshape(ns, bins, 2, depth, width),)
        in_specs, scratch = [pl.BlockSpec(memory_space=pl.ANY)], []
    place = pltpu.VMEM if fused else pl.ANY
    results = pl.pallas_call(
        functools.partial(gather_kernel, ns, np_, factor, fused),
        out_shape=[pltpu.VMEM(n, jnp.bfloat16) if fused else jax.ShapeDtypeStruct(n, jnp.bfloat16) for n in shapes],
        in_specs=in_specs,
        out_specs=[pl.BlockSpec(memory_space=place)] * len(shapes),
        scratch_shapes=scratch + [
            pltpu.SemaphoreType.DMA((ns,)),
            pltpu.SemaphoreType.DMA((np_, ns)),
            pltpu.SemaphoreType.DMA((np_, ns)),
            pltpu.SemaphoreType.DMA((np_, ns)),
            pltpu.SemaphoreType.DMA,
        ],
        compiler_params=pltpu.CompilerParams(
            collective_id=0, has_side_effects=True, vmem_limit_bytes=16 * 2**20),
    )(*operands)
    if fused:
        return finish(np_, factor, *results)
    return gram(results[0], factor)


def solution(mesh):
    return jax.shard_map(
        functools.partial(shards, mesh.shape["shot"], mesh.shape["pair"]),
        mesh=mesh,
        in_specs=(P(None, "shot", None, "pair"), P("shot")),
        out_specs=P(None, "shot", "pair", None),
        check_vma=False,
    )
```

```python
import functools

import jax
import jax.numpy as jnp
from jax import lax
from jax.experimental import pallas as pl
from jax.experimental.pallas import tpu as pltpu
from jax.sharding import PartitionSpec as P

MESH = pl.DeviceIdType.MESH


def meet(me, step, count):
    out, bit = 0, 1
    while bit < count:
        out = out + ((me // bit + step // bit) % 2) * bit
        bit *= 2
    return out


def put_left(f, p, g_ref, left_ref):
    width = g_ref.shape[-1]
    rows = g_ref[p, :, f]
    swapped = jnp.concatenate([-rows[:, 1:2], rows[:, 0:1]], axis=1)
    left = jnp.concatenate([rows.reshape(-1, width), swapped.reshape(-1, width)], axis=1)
    left_ref[f] = left.T


def block_product(f, q, g_ref, left_ref, factor):
    width = g_ref.shape[-1]
    right = g_ref[q, :, f].reshape(-1, width)
    return (jnp.dot(left_ref[f], right, preferred_element_type=jnp.float32) * factor).astype(jnp.bfloat16)


def prepare(t, j, raw_ref, weight_ref, wide_ref, x_ref):
    _, _, depth, bins, width = raw_ref.shape
    for c in range(2):
        for k in range(depth):
            scaled = raw_ref[t, c, k].astype(jnp.float32) * weight_ref[k]
            for h in range(width // 128):
                wide_ref[h, pl.ds((c * depth + k) * bins, bins), :] = scaled[:, h * 128:(h + 1) * 128]
    for c in range(2):
        for f in range(bins):
            for h in range(width // 128):
                shots = wide_ref[h, pl.ds(c * depth * bins + f, depth, stride=bins), :]
                x_ref[j, f, c, :, h * 128:(h + 1) * 128] = shots.astype(jnp.bfloat16)


def gather_kernel(ns, np_, factor, fused, *refs):
    if fused:
        spectra_ref, shot_weight_ref, g_ref, left_ref, o_ref, x_ref, raw_ref, wide_ref, weight_ref, load_sem, weight_sem, *sems = refs
    else:
        x_ref, g_ref, *sems = refs
    a2a_sem, up_sem, down_sem, recv_sem, own_sem = sems
    s, p = lax.axis_index("shot"), lax.axis_index("pair")
    bins, width = g_ref.shape[2], g_ref.shape[-1]
    share = -(-bins // ns)
    has_up, has_down = p < np_ - 1, p > 0

    def load(t):
        first_bin = pl.multiple_of(meet(s, t, ns) * bins, bins)
        return pltpu.make_async_copy(spectra_ref.at[:, :, pl.ds(first_bin, bins), :], raw_ref.at[t], load_sem.at[t])

    if fused:
        weights = pltpu.make_async_copy(shot_weight_ref, weight_ref, weight_sem)
        load(0).start()
        weights.start()
        for t in range(1, ns):
            load(t).start()

    barrier = pltpu.get_barrier_semaphore()

    def hello(t, carry):
        pl.semaphore_signal(barrier, inc=1, device_id=(meet(s, t, ns), p), device_id_type=MESH)
        return carry

    lax.fori_loop(1, ns, hello, 0)

    @pl.when(has_up)
    def _():
        pl.semaphore_signal(barrier, inc=1, device_id=(s, p + 1), device_id_type=MESH)

    @pl.when(has_down)
    def _():
        pl.semaphore_signal(barrier, inc=1, device_id=(s, p - 1), device_id_type=MESH)

    def ready(t):
        load(t).wait()
        prepare(t, meet(s, t, ns), raw_ref, weight_ref, wide_ref, x_ref)

    if fused:
        weights.wait()
        lax.fori_loop(0, min(2, ns), lambda t, carry: (ready(t), carry)[1], 0)

    pl.semaphore_wait(barrier, ns - 1 + has_up.astype(jnp.int32) + has_down.astype(jnp.int32))

    def up(q, j, src):
        return pltpu.make_async_remote_copy(
            src_ref=src, dst_ref=g_ref.at[q, j], send_sem=up_sem.at[q, j],
            recv_sem=recv_sem.at[q, j], device_id=(s, p + 1), device_id_type=MESH)

    def down(q, j, src):
        return pltpu.make_async_remote_copy(
            src_ref=src, dst_ref=g_ref.at[q, j], send_sem=down_sem.at[q, j],
            recv_sem=recv_sem.at[q, j], device_id=(s, p - 1), device_id_type=MESH)

    def exchange(t):
        j = meet(s, t, ns)
        return pltpu.make_async_remote_copy(
            src_ref=x_ref.at[j], dst_ref=g_ref.at[p, s], send_sem=a2a_sem.at[t],
            recv_sem=recv_sem.at[p, s], device_id=(j, p), device_id_type=MESH)

    def arrived(q, j):
        pltpu.make_async_copy(g_ref.at[q, j], g_ref.at[q, j], recv_sem.at[q, j]).wait()

    own = pltpu.make_async_copy(x_ref.at[s], g_ref.at[p, s], own_sem)

    @pl.when(has_up)
    def _():
        up(p, s, x_ref.at[s]).start()

    @pl.when(has_down)
    def _():
        down(p, s, x_ref.at[s]).start()

    def send(t, carry):
        if fused:
            @pl.when(t + 1 < ns)
            def _():
                ready(t + 1)

        exchange(t).start()
        return carry

    lax.fori_loop(1, ns, send, 0)
    own.start()

    def first(t, carry):
        j = meet(s, t, ns)
        arrived(p, j)

        @pl.when(has_up)
        def _():
            up(p, j, g_ref.at[p, j]).start()

        @pl.when(has_down)
        def _():
            down(p, j, g_ref.at[p, j]).start()

        return carry

    lax.fori_loop(1, ns, first, 0)

    own.wait()

    def exchanged(t, carry):
        exchange(t).wait_send()
        return carry

    lax.fori_loop(1, ns, exchanged, 0)

    def collect(r, j):
        @pl.when(has_up & (p >= r))
        def _():
            up(p - r, j, g_ref.at[p - r, j]).wait_send()

        @pl.when(has_down & (p + r < np_))
        def _():
            down(p + r, j, g_ref.at[p + r, j]).wait_send()

    def multiply(f, q):
        product = block_product(f, q, g_ref, left_ref, factor)
        columns = pl.ds(pl.multiple_of(q * width, width), width)
        o_ref[0, f, :, columns] = product[:width]
        o_ref[1, f, :, columns] = product[width:]

    def compute(r, t):
        def one_bin(f, carry):
            @pl.when(r == 0)
            def _():
                put_left(f, p, g_ref, left_ref)
                multiply(f, p)

            @pl.when((r > 0) & (p >= r))
            def _():
                multiply(f, p - r)

            @pl.when((r > 0) & (p + r < np_))
            def _():
                multiply(f, p + r)

            return carry

        lax.fori_loop(jnp.minimum(t * share, bins), jnp.minimum((t + 1) * share, bins), one_bin, 0)

    def relay(i, carry):
        r, j = i // ns, meet(s, i % ns, ns)
        if fused:
            compute(r - 1, i % ns)

        @pl.when(r > 1)
        def _():
            collect(r - 2, j)

        @pl.when(p >= r)
        def _():
            arrived(p - r, j)

            @pl.when(has_up)
            def _():
                up(p - r, j, g_ref.at[p - r, j]).start()

        @pl.when(p + r < np_)
        def _():
            arrived(p + r, j)

            @pl.when(has_down)
            def _():
                down(p + r, j, g_ref.at[p + r, j]).start()

        return carry

    lax.fori_loop(ns, np_ * ns, relay, 0)

    def rest(i, carry):
        collect(i // ns, i % ns)
        return carry

    lax.fori_loop(max(np_ - 2, 0) * ns, np_ * ns, rest, 0)


def finish_kernel(np_, factor, g_ref, left_ref, o_ref, out_ref, last_ref, done_sem, last_sem):
    p = lax.axis_index("pair")
    bins, width = g_ref.shape[2], g_ref.shape[-1]
    at_end = (p == 0) | (p == np_ - 1)
    q = np_ - 1 - p

    def whole(f):
        return pltpu.make_async_copy(o_ref.at[:, f], out_ref.at[:, f], done_sem.at[f])

    def most(f):
        columns = pl.ds(pl.multiple_of(jnp.where(p == 0, 0, width), width), (np_ - 1) * width)
        return pltpu.make_async_copy(o_ref.at[:, f, :, columns], out_ref.at[:, f, :, columns], done_sem.at[f])

    def last(f):
        columns = pl.ds(pl.multiple_of(q * width, width), width)
        return pltpu.make_async_copy(last_ref.at[:, f], out_ref.at[:, f, :, columns], last_sem.at[f])

    @pl.when(at_end)
    def _():
        for f in range(bins):
            most(f).start()
        for f in range(bins):
            product = block_product(f, q, g_ref, left_ref, factor)
            last_ref[0, f] = product[:width]
            last_ref[1, f] = product[width:]
            if f > 0:
                last(f - 1).start()
        last(bins - 1).start()
        for f in range(bins):
            most(f).wait()
            last(f).wait()

    @pl.when(jnp.logical_not(at_end))
    def _():
        for f in range(bins):
            whole(f).start()
        for f in range(bins):
            whole(f).wait()


def finish(np_, factor, gathered, left, products):
    _, bins, width, columns = products.shape
    return pl.pallas_call(
        functools.partial(finish_kernel, np_, factor),
        out_shape=jax.ShapeDtypeStruct(products.shape, jnp.bfloat16),
        in_specs=[pl.BlockSpec(memory_space=pltpu.VMEM)] * 3,
        out_specs=pl.BlockSpec(memory_space=pl.ANY),
        scratch_shapes=[
            pltpu.VMEM((2, bins, width, width), jnp.bfloat16),
            pltpu.SemaphoreType.DMA((bins,)),
            pltpu.SemaphoreType.DMA((bins,)),
        ],
        compiler_params=pltpu.CompilerParams(vmem_limit_bytes=16 * 2**20),
    )(*(pltpu.with_memory_space_constraint(a, pltpu.VMEM) for a in (gathered, left, products)))


def gram(gathered, factor):
    np_, ns, bins, _, depth, width = gathered.shape
    rows = lax.dynamic_index_in_dim(gathered, lax.axis_index("pair"), 0, keepdims=False)
    left = jnp.stack([rows, jnp.stack([-rows[:, :, 1], rows[:, :, 0]], axis=2)])
    product = jnp.einsum("ojfcsa,qjfcsb->ofaqb", left, gathered, preferred_element_type=jnp.float32)
    return (product * factor).astype(jnp.bfloat16).reshape(2, bins, width, np_ * width)


def shards(ns, np_, spectra, shot_weight):
    _, depth, freqs, width = spectra.shape
    bins = freqs // ns
    factor = (depth * ns) ** -0.5
    fused = width % 128 == 0 and bins % 16 == 0 and depth % 16 == 0
    shapes = [(np_, ns, bins, 2, depth, width)]
    if fused:
        shapes += [(bins, 2 * width, ns * 2 * depth), (2, bins, width, np_ * width)]
        operands = tuple(pltpu.with_memory_space_constraint(a, pltpu.HBM) for a in (spectra, shot_weight))
        in_specs = [pl.BlockSpec(memory_space=pltpu.HBM), pl.BlockSpec(memory_space=pltpu.HBM)]
        scratch = [
            pltpu.VMEM((ns, bins, 2, depth, width), jnp.bfloat16),
            pltpu.VMEM((ns, 2, depth, bins, width), jnp.bfloat16),
            pltpu.VMEM((width // 128, 2 * depth * bins, 128), jnp.float32),
            pltpu.SMEM((depth,), jnp.float32),
            pltpu.SemaphoreType.DMA((ns,)),
            pltpu.SemaphoreType.DMA,
        ]
    else:
        scaled = (spectra.astype(jnp.float32) * shot_weight[None, :, None, None]).astype(jnp.bfloat16)
        operands = (scaled.transpose(2, 0, 1, 3).reshape(ns, bins, 2, depth, width),)
        in_specs, scratch = [pl.BlockSpec(memory_space=pl.ANY)], []
    place = pltpu.VMEM if fused else pl.ANY
    results = pl.pallas_call(
        functools.partial(gather_kernel, ns, np_, factor, fused),
        out_shape=[pltpu.VMEM(n, jnp.bfloat16) if fused else jax.ShapeDtypeStruct(n, jnp.bfloat16) for n in shapes],
        in_specs=in_specs,
        out_specs=[pl.BlockSpec(memory_space=place)] * len(shapes),
        scratch_shapes=scratch + [
            pltpu.SemaphoreType.DMA((ns,)),
            pltpu.SemaphoreType.DMA((np_, ns)),
            pltpu.SemaphoreType.DMA((np_, ns)),
            pltpu.SemaphoreType.DMA((np_, ns)),
            pltpu.SemaphoreType.DMA,
        ],
        compiler_params=pltpu.CompilerParams(
            collective_id=0, has_side_effects=True, vmem_limit_bytes=16 * 2**20),
    )(*operands)
    if fused:
        return finish(np_, factor, *results)
    return gram(results[0], factor)


def solution(mesh):
    return jax.shard_map(
        functools.partial(shards, mesh.shape["shot"], mesh.shape["pair"]),
        mesh=mesh,
        in_specs=(P(None, "shot", None, "pair"), P("shot")),
        out_specs=P(None, "shot", "pair", None),
        check_vma=False,
    )
```

```python
import functools

import jax
import jax.numpy as jnp
from jax import lax
from jax.experimental import pallas as pl
from jax.experimental.pallas import tpu as pltpu
from jax.sharding import PartitionSpec as P

MESH = pl.DeviceIdType.MESH


def meet(me, step, count):
    out, bit = 0, 1
    while bit < count:
        out = out + ((me // bit + step // bit) % 2) * bit
        bit *= 2
    return out


def put_left(f, p, g_ref, left_ref):
    width = g_ref.shape[-1]
    rows = g_ref[p, :, f]
    swapped = jnp.concatenate([-rows[:, 1:2], rows[:, 0:1]], axis=1)
    left = jnp.concatenate([rows.reshape(-1, width), swapped.reshape(-1, width)], axis=1)
    left_ref[f] = left.T


def block_product(f, q, g_ref, left_ref, factor):
    width = g_ref.shape[-1]
    right = g_ref[q, :, f].reshape(-1, width)
    return (jnp.dot(left_ref[f], right, preferred_element_type=jnp.float32) * factor).astype(jnp.bfloat16)


def widen(t, raw_ref, weight_ref, wide_ref):
    _, _, depth, bins, width = raw_ref.shape
    for c in range(2):
        for k in range(depth):
            scaled = raw_ref[t, c, k].astype(jnp.float32) * weight_ref[k]
            for h in range(width // 128):
                wide_ref[h, pl.ds((c * depth + k) * bins, bins), :] = scaled[:, h * 128:(h + 1) * 128]


def narrow(j, wide_ref, x_ref):
    _, bins, _, depth, width = x_ref.shape
    for c in range(2):
        for f in range(bins):
            for h in range(width // 128):
                shots = wide_ref[h, pl.ds(c * depth * bins + f, depth, stride=bins), :]
                x_ref[j, f, c, :, h * 128:(h + 1) * 128] = shots.astype(jnp.bfloat16)


def gather_kernel(ns, np_, factor, fused, *refs):
    if fused:
        spectra_ref, shot_weight_ref, g_ref, left_ref, o_ref, x_ref, raw_ref, wide_ref, weight_ref, load_sem, weight_sem, *sems = refs
    else:
        x_ref, g_ref, *sems = refs
    a2a_sem, up_sem, down_sem, recv_sem, own_sem = sems
    s, p = lax.axis_index("shot"), lax.axis_index("pair")
    bins, width = g_ref.shape[2], g_ref.shape[-1]
    share = -(-bins // ns)
    has_up, has_down = p < np_ - 1, p > 0

    def load(t):
        first_bin = pl.multiple_of(meet(s, t, ns) * bins, bins)
        return pltpu.make_async_copy(spectra_ref.at[:, :, pl.ds(first_bin, bins), :], raw_ref.at[t], load_sem.at[t])

    if fused:
        weights = pltpu.make_async_copy(shot_weight_ref, weight_ref, weight_sem)
        load(0).start()
        weights.start()
        for t in range(1, ns):
            load(t).start()

    barrier = pltpu.get_barrier_semaphore()

    def hello(t, carry):
        pl.semaphore_signal(barrier, inc=1, device_id=(meet(s, t, ns), p), device_id_type=MESH)
        return carry

    lax.fori_loop(1, ns, hello, 0)

    @pl.when(has_up)
    def _():
        pl.semaphore_signal(barrier, inc=1, device_id=(s, p + 1), device_id_type=MESH)

    @pl.when(has_down)
    def _():
        pl.semaphore_signal(barrier, inc=1, device_id=(s, p - 1), device_id_type=MESH)

    def ready(t):
        load(t).wait()
        widen(t, raw_ref, weight_ref, wide_ref)
        narrow(meet(s, t, ns), wide_ref, x_ref)

    if fused:
        weights.wait()
        ready(0)
        if ns > 1:
            load(1).wait()
            widen(1, raw_ref, weight_ref, wide_ref)

    pl.semaphore_wait(barrier, ns - 1 + has_up.astype(jnp.int32) + has_down.astype(jnp.int32))

    def up(q, j, src):
        return pltpu.make_async_remote_copy(
            src_ref=src, dst_ref=g_ref.at[q, j], send_sem=up_sem.at[q, j],
            recv_sem=recv_sem.at[q, j], device_id=(s, p + 1), device_id_type=MESH)

    def down(q, j, src):
        return pltpu.make_async_remote_copy(
            src_ref=src, dst_ref=g_ref.at[q, j], send_sem=down_sem.at[q, j],
            recv_sem=recv_sem.at[q, j], device_id=(s, p - 1), device_id_type=MESH)

    def exchange(t):
        j = meet(s, t, ns)
        return pltpu.make_async_remote_copy(
            src_ref=x_ref.at[j], dst_ref=g_ref.at[p, s], send_sem=a2a_sem.at[t],
            recv_sem=recv_sem.at[p, s], device_id=(j, p), device_id_type=MESH)

    def arrived(q, j):
        pltpu.make_async_copy(g_ref.at[q, j], g_ref.at[q, j], recv_sem.at[q, j]).wait()

    own = pltpu.make_async_copy(x_ref.at[s], g_ref.at[p, s], own_sem)

    @pl.when(has_up)
    def _():
        up(p, s, x_ref.at[s]).start()

    @pl.when(has_down)
    def _():
        down(p, s, x_ref.at[s]).start()

    if fused and ns > 1:
        narrow(meet(s, 1, ns), wide_ref, x_ref)

    def send(t, carry):
        if fused:
            @pl.when(t + 1 < ns)
            def _():
                ready(t + 1)

        exchange(t).start()
        return carry

    lax.fori_loop(1, ns, send, 0)
    own.start()

    def first(t, carry):
        j = meet(s, t, ns)
        arrived(p, j)

        @pl.when(has_up)
        def _():
            up(p, j, g_ref.at[p, j]).start()

        @pl.when(has_down)
        def _():
            down(p, j, g_ref.at[p, j]).start()

        return carry

    lax.fori_loop(1, ns, first, 0)

    own.wait()

    def exchanged(t, carry):
        exchange(t).wait_send()
        return carry

    lax.fori_loop(1, ns, exchanged, 0)

    def collect(r, j):
        @pl.when(has_up & (p >= r))
        def _():
            up(p - r, j, g_ref.at[p - r, j]).wait_send()

        @pl.when(has_down & (p + r < np_))
        def _():
            down(p + r, j, g_ref.at[p + r, j]).wait_send()

    def multiply(f, q):
        product = block_product(f, q, g_ref, left_ref, factor)
        columns = pl.ds(pl.multiple_of(q * width, width), width)
        o_ref[0, f, :, columns] = product[:width]
        o_ref[1, f, :, columns] = product[width:]

    def compute(r, t):
        def one_bin(f, carry):
            @pl.when(r == 0)
            def _():
                put_left(f, p, g_ref, left_ref)
                multiply(f, p)

            @pl.when((r > 0) & (p >= r))
            def _():
                multiply(f, p - r)

            @pl.when((r > 0) & (p + r < np_))
            def _():
                multiply(f, p + r)

            return carry

        lax.fori_loop(jnp.minimum(t * share, bins), jnp.minimum((t + 1) * share, bins), one_bin, 0)

    def relay(i, carry):
        r, j = i // ns, meet(s, i % ns, ns)
        if fused:
            compute(r - 1, i % ns)

        @pl.when(r > 1)
        def _():
            collect(r - 2, j)

        @pl.when(p >= r)
        def _():
            arrived(p - r, j)

            @pl.when(has_up)
            def _():
                up(p - r, j, g_ref.at[p - r, j]).start()

        @pl.when(p + r < np_)
        def _():
            arrived(p + r, j)

            @pl.when(has_down)
            def _():
                down(p + r, j, g_ref.at[p + r, j]).start()

        return carry

    lax.fori_loop(ns, np_ * ns, relay, 0)

    def rest(i, carry):
        collect(i // ns, i % ns)
        return carry

    lax.fori_loop(max(np_ - 2, 0) * ns, np_ * ns, rest, 0)


def finish_kernel(np_, factor, g_ref, left_ref, o_ref, out_ref, last_ref, done_sem, last_sem):
    p = lax.axis_index("pair")
    bins, width = g_ref.shape[2], g_ref.shape[-1]
    at_end = (p == 0) | (p == np_ - 1)
    q = np_ - 1 - p

    def whole(f):
        return pltpu.make_async_copy(o_ref.at[:, f], out_ref.at[:, f], done_sem.at[f])

    def most(f):
        columns = pl.ds(pl.multiple_of(jnp.where(p == 0, 0, width), width), (np_ - 1) * width)
        return pltpu.make_async_copy(o_ref.at[:, f, :, columns], out_ref.at[:, f, :, columns], done_sem.at[f])

    def last(f):
        columns = pl.ds(pl.multiple_of(q * width, width), width)
        return pltpu.make_async_copy(last_ref.at[:, f], out_ref.at[:, f, :, columns], last_sem.at[f])

    @pl.when(at_end)
    def _():
        for f in range(bins):
            most(f).start()
        for f in range(bins):
            product = block_product(f, q, g_ref, left_ref, factor)
            last_ref[0, f] = product[:width]
            last_ref[1, f] = product[width:]
            if f > 0:
                last(f - 1).start()
        last(bins - 1).start()
        for f in range(bins):
            most(f).wait()
            last(f).wait()

    @pl.when(jnp.logical_not(at_end))
    def _():
        for f in range(bins):
            whole(f).start()
        for f in range(bins):
            whole(f).wait()


def finish(np_, factor, gathered, left, products):
    _, bins, width, columns = products.shape
    return pl.pallas_call(
        functools.partial(finish_kernel, np_, factor),
        out_shape=jax.ShapeDtypeStruct(products.shape, jnp.bfloat16),
        in_specs=[pl.BlockSpec(memory_space=pltpu.VMEM)] * 3,
        out_specs=pl.BlockSpec(memory_space=pl.ANY),
        scratch_shapes=[
            pltpu.VMEM((2, bins, width, width), jnp.bfloat16),
            pltpu.SemaphoreType.DMA((bins,)),
            pltpu.SemaphoreType.DMA((bins,)),
        ],
        compiler_params=pltpu.CompilerParams(vmem_limit_bytes=16 * 2**20),
    )(*(pltpu.with_memory_space_constraint(a, pltpu.VMEM) for a in (gathered, left, products)))


def gram(gathered, factor):
    np_, ns, bins, _, depth, width = gathered.shape
    rows = lax.dynamic_index_in_dim(gathered, lax.axis_index("pair"), 0, keepdims=False)
    left = jnp.stack([rows, jnp.stack([-rows[:, :, 1], rows[:, :, 0]], axis=2)])
    product = jnp.einsum("ojfcsa,qjfcsb->ofaqb", left, gathered, preferred_element_type=jnp.float32)
    return (product * factor).astype(jnp.bfloat16).reshape(2, bins, width, np_ * width)


def shards(ns, np_, spectra, shot_weight):
    _, depth, freqs, width = spectra.shape
    bins = freqs // ns
    factor = (depth * ns) ** -0.5
    fused = width % 128 == 0 and bins % 16 == 0 and depth % 16 == 0
    shapes = [(np_, ns, bins, 2, depth, width)]
    if fused:
        shapes += [(bins, 2 * width, ns * 2 * depth), (2, bins, width, np_ * width)]
        operands = tuple(pltpu.with_memory_space_constraint(a, pltpu.HBM) for a in (spectra, shot_weight))
        in_specs = [pl.BlockSpec(memory_space=pltpu.HBM), pl.BlockSpec(memory_space=pltpu.HBM)]
        scratch = [
            pltpu.VMEM((ns, bins, 2, depth, width), jnp.bfloat16),
            pltpu.VMEM((ns, 2, depth, bins, width), jnp.bfloat16),
            pltpu.VMEM((width // 128, 2 * depth * bins, 128), jnp.float32),
            pltpu.SMEM((depth,), jnp.float32),
            pltpu.SemaphoreType.DMA((ns,)),
            pltpu.SemaphoreType.DMA,
        ]
    else:
        scaled = (spectra.astype(jnp.float32) * shot_weight[None, :, None, None]).astype(jnp.bfloat16)
        operands = (scaled.transpose(2, 0, 1, 3).reshape(ns, bins, 2, depth, width),)
        in_specs, scratch = [pl.BlockSpec(memory_space=pl.ANY)], []
    place = pltpu.VMEM if fused else pl.ANY
    results = pl.pallas_call(
        functools.partial(gather_kernel, ns, np_, factor, fused),
        out_shape=[pltpu.VMEM(n, jnp.bfloat16) if fused else jax.ShapeDtypeStruct(n, jnp.bfloat16) for n in shapes],
        in_specs=in_specs,
        out_specs=[pl.BlockSpec(memory_space=place)] * len(shapes),
        scratch_shapes=scratch + [
            pltpu.SemaphoreType.DMA((ns,)),
            pltpu.SemaphoreType.DMA((np_, ns)),
            pltpu.SemaphoreType.DMA((np_, ns)),
            pltpu.SemaphoreType.DMA((np_, ns)),
            pltpu.SemaphoreType.DMA,
        ],
        compiler_params=pltpu.CompilerParams(
            collective_id=0, has_side_effects=True, vmem_limit_bytes=16 * 2**20),
    )(*operands)
    if fused:
        return finish(np_, factor, *results)
    return gram(results[0], factor)


def solution(mesh):
    return jax.shard_map(
        functools.partial(shards, mesh.shape["shot"], mesh.shape["pair"]),
        mesh=mesh,
        in_specs=(P(None, "shot", None, "pair"), P("shot")),
        out_specs=P(None, "shot", "pair", None),
        check_vma=False,
    )
```
